32 devices in a mesh: span: 16 (over z, y, x), wall: 2 (over core).
Axes of the slice: x: 2, y: 2, z: 4, core: 2. Of those that a mesh axis runs over, the one named last changes fastest.
Arguments:
- velocity: bfloat16 [64, 3, 8, 128, 256], P(None, None, None, 'span', 'wall'), may hold values from -1080 to 1080, as said below
- wall_metric: float32 [256], P('wall'), may hold values from 0.5 to 2
Outputs:
- modes: bfloat16 [64, 3, 2, 128, 256], P(None, None, None, 'span', 'wall')
- r_factor: float32 [64, 64], replicated
The draws below stay inside these ranges and needn't reach their ends.
Inputs may be any that keep to these rules, and one draw needn't show every extreme that they name: velocity fields of order up to a few hundred.
All inputs are finite; a program needn't handle non-finite values.
Results may differ from the reference program's by a relative error of at most 0.0063.
Values may be sent and summed in bfloat16 or wider, within the bound.
A program may use at most 64 MiB of HBM per device.

```python
import math
import jax
import jax.numpy as jnp
from jax import lax

M = 64
XP = 2
NZ = 128
NY = 256
NROW = 196608


def draw_velocity(key, part):
    shape = (M, 3, XP + 6, NZ, NY)
    common_key = jax.random.fold_in(key, 11)
    own_key = jax.random.fold_in(key, 12)
    scale_key = jax.random.fold_in(key, 13)
    rough_key = jax.random.fold_in(key, 14)
    common = jnp.clip(jax.random.normal(common_key, (1, 3, XP + 6, NZ, NY), jnp.float32), -5.0, 5.0)
    own = jnp.clip(jax.random.normal(own_key, shape, jnp.float32), -5.0, 5.0)
    span_rise = 1.0 + 2.0 * jnp.arange(NZ, dtype=jnp.float32) / NZ
    wall_rise = 1.0 + 2.0 * jnp.arange(NY, dtype=jnp.float32) / NY
    scales = jnp.exp(jax.random.uniform(scale_key, (M, 1, 1, 1, 1), jnp.float32, 0.0, 2.302585))
    rough = jax.random.uniform(rough_key, (1, 1, 1, NZ, NY), jnp.float32, 0.6, 1.5)
    envelope = span_rise[:, None] * wall_rise[None, :] * rough
    return (scales * envelope * (0.6 * common + own)).astype(jnp.bfloat16)


def block_levels(rng, shape, split, least, largest):
    level = 1.0
    for position, parts in split:
        heights = jax.random.uniform(jax.random.fold_in(jax.random.fold_in(rng, 6), position), (parts,), jnp.float32, least / len(split), largest / len(split))
        level = level * jnp.repeat(jnp.exp(heights), shape[position] // parts).reshape((-1,) + (1,) * (len(shape) - 1 - position))
    return level


def setup_inputs(seed: int = 0) -> dict:
    key_of = jax.random.split(jax.random.key(seed), 3)
    return {
        "velocity": draw_velocity(jax.random.fold_in(key_of[2], 71), 0),
        "wall_metric": jnp.clip(jnp.exp(math.log(2.0) - 1.3862944 * jax.random.uniform(key_of[1], (NY,), jnp.float32) ** block_levels(key_of[1], (NY,), ((0, 2),), -0.2, 0.2)), 0.5, 2.0),
    }


def stencil(padded, axis, length):

    def take(k):
        return lax.slice_in_dim(padded, 3 + k, 3 + k + length, axis=axis).astype(jnp.float32)
    return (45.0 * (take(1) - take(-1)) - 9.0 * (take(2) - take(-2)) + (take(3) - take(-3))) / 60.0

def factor_lower(gram):
    order = gram.shape[0]
    positions = jnp.arange(order, dtype=jnp.int32)

    def column(index, lower):
        at = jnp.asarray(index).astype(jnp.int32)
        above = lax.dynamic_slice_in_dim(gram, at, 1, 1)[:, 0]
        row_j = lax.dynamic_slice_in_dim(lower, at, 1, 0)[0]
        rest = above - lax.optimization_barrier(jnp.sum(lower * row_j[None, :], axis=1))
        pivot = jnp.sqrt(lax.dynamic_slice_in_dim(rest, at, 1, 0)[0])
        keep = (positions >= at).astype(gram.dtype)
        pick = (positions == at).astype(gram.dtype)
        return lower + (keep * rest / pivot)[:, None] * pick[None, :]
    return lax.fori_loop(0, order, column, jnp.zeros_like(gram))

def invert_lower(lower):
    order = lower.shape[0]
    positions = jnp.arange(order, dtype=jnp.int32)

    def row_step(index, inverse):
        at = jnp.asarray(index).astype(jnp.int32)
        pick = (positions == at).astype(lower.dtype)
        row_l = lax.dynamic_slice_in_dim(lower, at, 1, 0)[0]
        pivot = lax.dynamic_slice_in_dim(row_l, at, 1, 0)[0]
        new_row = (pick - lax.optimization_barrier(jnp.sum(row_l[:, None] * inverse, axis=0))) / pivot
        return inverse + pick[:, None] * new_row[None, :]
    return lax.fori_loop(0, order, row_step, jnp.zeros_like(lower))

def reference(velocity, wall_metric):

    def single(snap):
        inner = snap[:, 3:3 + XP]
        zpad = jnp.concatenate([inner[:, :, -3:, :], inner, inner[:, :, :3, :]], axis=2)
        ypad = jnp.pad(inner, ((0, 0), (0, 0), (0, 0), (3, 3)))
        du_dz = stencil(zpad[0], 1, NZ)
        dv_dz = stencil(zpad[1], 1, NZ)
        du_dy = wall_metric * stencil(ypad[0], 2, NY)
        dw_dy = wall_metric * stencil(ypad[2], 2, NY)
        dv_dx = stencil(snap[1], 0, XP)
        dw_dx = stencil(snap[2], 0, XP)
        return jnp.stack([dw_dy - dv_dz, du_dz - dw_dx, dv_dx - du_dy], axis=0).astype(jnp.bfloat16)
    vorticity = lax.map(single, velocity)
    flat = vorticity.reshape(M, -1)
    gram = jnp.dot(flat, flat.T, preferred_element_type=jnp.float32) / NROW
    lower = factor_lower(gram)
    upper = lower.T
    r_inverse = invert_lower(lower).T.astype(jnp.bfloat16)
    modes = jnp.dot(r_inverse.T, flat, preferred_element_type=jnp.float32).astype(jnp.bfloat16)
    return (modes.reshape(vorticity.shape), upper)
```

```python
import functools

import jax
import jax.numpy as jnp
import ml_dtypes
import numpy as np
from jax import lax
from jax.experimental import pallas as pl
from jax.experimental.pallas import tpu as pltpu
from jax.sharding import PartitionSpec as P

MESH = pl.DeviceIdType.MESH
BF = jnp.bfloat16
F32 = jnp.float32


def coef(offset):
    table = {1: 45.0, 2: -9.0, 3: 1.0}
    size = np.abs(offset)
    out = np.zeros(offset.shape, np.float32)
    for step, value in table.items():
        out = np.where(size == step, value * np.sign(offset), out)
    return out


def constants(snaps, cells, lanes, planes, block):
    groups = block * planes
    z = np.arange(cells)
    r = np.arange(3)
    eye = np.eye(groups, dtype=np.float32)
    pick = np.stack(
        [
            np.kron(eye, (z[None, :] == r[:, None]).astype(np.float32)),
            np.kron(eye, (z[None, :] == cells - 3 + r[:, None]).astype(np.float32)),
        ]
    )
    span = np.concatenate(
        [
            np.kron(eye, coef(z[None, :] - z[:, None])),
            np.kron(eye, coef(r[None, :] - 3 - z[:, None])),
            np.kron(eye, coef(cells + r[None, :] - z[:, None])),
        ],
        axis=1,
    )
    y = np.arange(lanes)
    diff = y[:, None] - y[None, :]
    wall = np.concatenate([coef(diff), coef(diff - lanes), coef(diff + lanes)], axis=0)
    owner = np.arange(snaps * cells) // cells
    one = (owner[:, None] == np.arange(snaps)[None, :]).astype(np.float32)
    fold = np.concatenate([one, one], axis=1)
    spread = np.concatenate([np.zeros_like(one.T), one.T], axis=0)
    return [jnp.asarray(a.astype(ml_dtypes.bfloat16)) for a in (pick, span, wall, fold, spread)]


def dot(a, b):
    return jnp.dot(a, b, preferred_element_type=F32)


def eliminate(rows):
    groups = list(rows)
    count = len(groups)
    sub = lax.broadcasted_iota(jnp.int32, (8, 128), 0)
    for j in range(8 * count):
        b, r = divmod(j, 8)
        pivot_row = jnp.broadcast_to(groups[b][r : r + 1, :], (8, 128))
        inv = 1.0 / jnp.broadcast_to(pivot_row[:, j : j + 1], (8, 128))
        scaled = pivot_row * inv
        for i in range(b, count):
            if i == b and r == 7:
                continue
            column = jnp.broadcast_to(groups[i][:, j : j + 1], (8, 128))
            if i == b:
                column = jnp.where(sub > r, column, 0.0)
            groups[i] = groups[i] - column * scaled
    return groups


def kernel(
    span_count, wall_count, total_rows,
    vel, metric_ref, pick_ref, span_ref, wall_ref, fold_ref, spread_ref,
    out_ref, r_ref,
    u_buf, vw_buf, send_buf, lo_buf, hi_buf, ylo_buf, yhi_buf, acc, vort, prod,
    wall_sum, span_sum,
    local_sem, hs_sem, hr_sem, ys_sem, yr_sem, ws_sem, wr_sem, ss_sem, sr_sem,
):
    snaps = vel.shape[0]
    planes = u_buf.shape[1]
    cells, lanes = vel.shape[3], vel.shape[4]
    block = 16
    rows = block * planes * cells
    edge = block * planes * 3
    blocks = snaps // block
    me = lax.axis_index("span")
    mw = lax.axis_index("wall")

    load_u = pltpu.make_async_copy(vel.at[:, 0, pl.ds(3, planes)], u_buf, local_sem.at[0])
    load_v = pltpu.make_async_copy(vel.at[:, 1], vw_buf.at[0], local_sem.at[1])
    load_w = pltpu.make_async_copy(vel.at[:, 2], vw_buf.at[1], local_sem.at[2])
    load_u.start()
    load_v.start()
    load_w.start()

    barrier = pltpu.get_barrier_semaphore()
    for d in range(1, span_count):
        pl.semaphore_signal(
            barrier, inc=1, device_id=(lax.rem(me + d, span_count), mw), device_id_type=MESH
        )
    for d in range(1, wall_count):
        pl.semaphore_signal(
            barrier, inc=1, device_id=(me, lax.rem(mw + d, wall_count)), device_id_type=MESH
        )

    def inner(c, k):
        at = pl.ds(k * block, block)
        if c == 0:
            value = u_buf[at]
        else:
            value = vw_buf[c - 1, at, pl.ds(3, planes)]
        return value.astype(F32).reshape(rows, lanes).astype(BF)

    load_u.wait()
    load_v.wait()
    for c in range(2):
        for k in range(blocks):
            f = inner(c, k)
            for side in range(2):
                send_buf[side, c, k * edge : (k + 1) * edge] = dot(pick_ref[side], f).astype(BF)
    load_w.wait()
    pl.semaphore_wait(barrier, span_count + wall_count - 2)

    down = lax.rem(me + span_count - 1, span_count)
    up = lax.rem(me + 1, span_count)
    halo = []
    for c in range(2):
        to_down = pltpu.make_async_remote_copy(
            send_buf.at[0, c], hi_buf.at[c], hs_sem.at[0, c], hr_sem.at[0, c],
            device_id=(down, mw), device_id_type=MESH,
        )
        to_up = pltpu.make_async_remote_copy(
            send_buf.at[1, c], lo_buf.at[c], hs_sem.at[1, c], hr_sem.at[1, c],
            device_id=(up, mw), device_id_type=MESH,
        )
        to_down.start()
        to_up.start()
        halo.append((to_down, to_up))

    wall_src = (u_buf, vw_buf.at[1, :, pl.ds(3, planes)])
    y_up = [
        pltpu.make_async_remote_copy(
            wall_src[c], ylo_buf.at[c], ys_sem.at[0, c], yr_sem.at[0, c],
            device_id=(me, lax.rem(mw + 1, wall_count)), device_id_type=MESH,
        )
        for c in range(2)
    ]
    y_down = [
        pltpu.make_async_remote_copy(
            wall_src[c], yhi_buf.at[c], ys_sem.at[1, c], yr_sem.at[1, c],
            device_id=(me, lax.rem(mw + wall_count - 1, wall_count)), device_id_type=MESH,
        )
        for c in range(2)
    ]

    @pl.when(mw < wall_count - 1)
    def _():
        for c in range(2):
            y_up[c].start()

    @pl.when(mw > 0)
    def _():
        for c in range(2):
            y_down[c].start()

    @pl.when(mw == 0)
    def _():
        ylo_buf[...] = jnp.zeros_like(ylo_buf)

    @pl.when(mw == wall_count - 1)
    def _():
        yhi_buf[...] = jnp.zeros_like(yhi_buf)

    def along_x(k, carry):
        at = pl.ds(k * 4, 4)
        for c in range(2):
            f = [vw_buf[c, at, q].astype(F32) for q in range(6 + planes)]
            for p in range(planes):
                d = (
                    45.0 * (f[p + 4] - f[p + 2]) - 9.0 * (f[p + 5] - f[p + 1])
                    + (f[p + 6] - f[p])
                )
                if c == 0:
                    acc[2, p, at] = d
                else:
                    acc[1, p, at] = -d
        return carry

    lax.fori_loop(0, snaps // 4, along_x, 0)

    @pl.when(mw > 0)
    def _():
        for c in range(2):
            y_up[c].wait_recv()

    @pl.when(mw < wall_count - 1)
    def _():
        for c in range(2):
            y_down[c].wait_recv()

    metric = metric_ref[...].reshape(1, 1, 1, lanes)
    for c in range(2):
        for k in range(blocks):
            at = pl.ds(k * block, block)
            f = inner(2 * c, k)
            low = ylo_buf[c, at].astype(F32).reshape(rows, lanes).astype(BF)
            high = yhi_buf[c, at].astype(F32).reshape(rows, lanes).astype(BF)
            d = dot(jnp.concatenate([f, low, high], axis=1), wall_ref[...])
            d = d.reshape(block, planes, cells, lanes) * metric
            for p in range(planes):
                if c == 0:
                    acc[2, p, at] = acc[2, p, at] - d[:, p]
                else:
                    acc[0, p, at] = d[:, p]

    def finish(comp, p, k, value):
        slab = comp * planes + p
        vort[k * block * cells : (k + 1) * block * cells, slab * lanes : (slab + 1) * lanes] = (
            (value * (1.0 / 60.0)).reshape(block * cells, lanes).astype(BF)
        )

    for k in range(blocks):
        at = pl.ds(k * block, block)
        for p in range(planes):
            finish(2, p, k, acc[2, p, at])
    for c in range(2):
        halo[c][0].wait_recv()
        halo[c][1].wait_recv()
        for k in range(blocks):
            at = pl.ds(k * block, block)
            part = slice(k * edge, (k + 1) * edge)
            stack = jnp.concatenate([inner(c, k), lo_buf[c, part], hi_buf[c, part]], axis=0)
            d = dot(span_ref[...], stack).reshape(block, planes, cells, lanes)
            for p in range(planes):
                if c == 0:
                    finish(1, p, k, acc[1, p, at] + d[:, p])
                else:
                    finish(0, p, k, acc[0, p, at] - d[:, p])

    wide = snaps * cells
    tiles = wide // 128
    lane_z = lax.rem(lax.broadcasted_iota(jnp.int32, (snaps, 128), 1), cells)
    parts = []
    for t in range(tiles):
        prod[t] = lax.dot_general(
            vort[...], vort[t * 128 : (t + 1) * 128],
            (((1,), (1,)), ((), ())), preferred_element_type=F32,
        )
        q = jnp.zeros((snaps, 128), F32)
        for z in range(cells):
            q = jnp.where(lane_z == z, prod[t, pl.ds(z, snaps, stride=cells), :], q)
        parts.append(q)
    q = jnp.concatenate(parts, axis=1)
    q1 = q.astype(BF)
    rest = q - q1.astype(F32)
    q2 = rest.astype(BF)
    q3 = (rest - q2.astype(F32)).astype(BF)
    g3 = dot(jnp.concatenate([q1, q2, q3], axis=0), fold_ref[...])
    g = g3[:snaps] + g3[snaps : 2 * snaps] + g3[2 * snaps :]
    half = snaps // 2
    lane = lax.broadcasted_iota(jnp.int32, (half, 2 * snaps), 1)
    packed = jnp.where(lane < snaps, g[:half], g[half:])

    wall_sum[mw] = packed
    copies = []
    for d in range(1, wall_count):
        copy = pltpu.make_async_remote_copy(
            wall_sum.at[mw], wall_sum.at[mw], ws_sem.at[d], wr_sem.at[d],
            device_id=(me, lax.rem(mw + d, wall_count)), device_id_type=MESH,
        )
        copy.start()
        copies.append(copy)
    for copy in copies:
        copy.wait_recv()
    total = wall_sum[0]
    for i in range(1, wall_count):
        total = total + wall_sum[i]
    span_sum[me] = total
    for d in range(1, span_count):
        copy = pltpu.make_async_remote_copy(
            span_sum.at[me], span_sum.at[me], ss_sem.at[d], sr_sem.at[d],
            device_id=(lax.rem(me + d, span_count), mw), device_id_type=MESH,
        )
        copy.start()
        copies.append(copy)
    for copy in copies[wall_count - 1 :]:
        copy.wait_recv()
    total = span_sum[0]
    for i in range(1, span_count):
        total = total + span_sum[i]
    gram = total / total_rows

    sub = lax.broadcasted_iota(jnp.int32, (half, 2 * snaps), 0)
    top = jnp.where(lane < snaps, gram, (lane - snaps == sub).astype(F32))
    bottom = jnp.where(
        lane < snaps, pltpu.roll(gram, snaps, 1), (lane - snaps - half == sub).astype(F32)
    )
    groups = [top[8 * i : 8 * i + 8] for i in range(half // 8)]
    groups += [bottom[8 * i : 8 * i + 8] for i in range(half // 8)]
    done = jnp.concatenate(eliminate(groups), axis=0)
    lane = lax.broadcasted_iota(jnp.int32, (snaps, 2 * snaps), 1)
    sub = lax.broadcasted_iota(jnp.int32, (snaps, 2 * snaps), 0)
    diagonal = jnp.sum(jnp.where(lane == sub, done, 0.0), axis=1, keepdims=True)
    done = jnp.where(lane < sub, 0.0, done / jnp.sqrt(diagonal))
    r_ref[...] = done[:, :snaps]

    x = dot(done.astype(BF), spread_ref[...]).astype(BF)
    full = dot(fold_ref[:, :snaps], x)
    row_z = lax.rem(lax.broadcasted_iota(jnp.int32, (wide, wide), 0), cells)
    col_z = lax.rem(lax.broadcasted_iota(jnp.int32, (wide, wide), 1), cells)
    weights = jnp.where(row_z == col_z, full, 0.0).astype(BF)
    for comp in range(3):
        for p in range(planes):
            slab = comp * planes + p
            m = dot(weights, vort[:, slab * lanes : (slab + 1) * lanes])
            out_ref[:, comp, p] = m.reshape(snaps, cells, lanes).astype(BF)

    for copy in copies:
        copy.wait_send()
    for pair in halo:
        for copy in pair:
            copy.wait_send()

    @pl.when(mw < wall_count - 1)
    def _():
        for c in range(2):
            y_up[c].wait_send()

    @pl.when(mw > 0)
    def _():
        for c in range(2):
            y_down[c].wait_send()


def per_device(velocity, wall_metric):
    snaps, comps, depth, cells, lanes = velocity.shape
    planes = depth - 6
    spans, walls = lax.axis_size("span"), lax.axis_size("wall")
    total_rows = 3 * planes * cells * spans * lanes * walls
    consts = constants(snaps, cells, lanes, planes, 16)
    vmem = pl.BlockSpec(memory_space=pltpu.VMEM)
    dma = pltpu.SemaphoreType.DMA
    edge = snaps * planes * 3
    wide = snaps * cells
    return pl.pallas_call(
        functools.partial(kernel, spans, walls, total_rows),
        out_shape=(
            jax.ShapeDtypeStruct((snaps, 3, planes, cells, lanes), BF),
            jax.ShapeDtypeStruct((snaps, snaps), F32),
        ),
        in_specs=[pl.BlockSpec(memory_space=pl.ANY)] + [vmem] * 6,
        out_specs=(vmem, vmem),
        scratch_shapes=[
            pltpu.VMEM((snaps, planes, cells, lanes), BF),
            pltpu.VMEM((2, snaps, depth, cells, lanes), BF),
            pltpu.VMEM((2, 2, edge, lanes), BF),
            pltpu.VMEM((2, edge, lanes), BF),
            pltpu.VMEM((2, edge, lanes), BF),
            pltpu.VMEM((2, snaps, planes, cells, lanes), BF),
            pltpu.VMEM((2, snaps, planes, cells, lanes), BF),
            pltpu.VMEM((3, planes, snaps, cells, lanes), F32),
            pltpu.VMEM((wide, 3 * planes * lanes), BF),
            pltpu.VMEM((wide // 128, wide, 128), F32),
            pltpu.VMEM((walls, snaps // 2, 2 * snaps), F32),
            pltpu.VMEM((spans, snaps // 2, 2 * snaps), F32),
            dma((3,)),
            dma((2, 2)),
            dma((2, 2)),
            dma((2, 2)),
            dma((2, 2)),
            dma((walls,)),
            dma((walls,)),
            dma((spans,)),
            dma((spans,)),
        ],
        compiler_params=pltpu.CompilerParams(
            collective_id=0, has_side_effects=True, vmem_limit_bytes=48 << 20
        ),
        name="pod",
    )(velocity, wall_metric.reshape(1, lanes), *consts)


def solution(mesh):
    in_specs = (P(None, None, None, "span", "wall"), P("wall"))
    out_specs = (P(None, None, None, "span", "wall"), P())
    return jax.shard_map(
        per_device, mesh=mesh, in_specs=in_specs, out_specs=out_specs, check_vma=False
    )
```

```python
import functools

import jax
import jax.numpy as jnp
import ml_dtypes
import numpy as np
from jax import lax
from jax.experimental import pallas as pl
from jax.experimental.pallas import tpu as pltpu
from jax.sharding import PartitionSpec as P

MESH = pl.DeviceIdType.MESH
BF = jnp.bfloat16
F32 = jnp.float32


def coef(offset):
    table = {1: 45.0, 2: -9.0, 3: 1.0}
    size = np.abs(offset)
    out = np.zeros(offset.shape, np.float32)
    for step, value in table.items():
        out = np.where(size == step, value * np.sign(offset), out)
    return out


def constants(snaps, cells, lanes, planes, block):
    groups = block * planes
    z = np.arange(cells)
    r = np.arange(3)
    eye = np.eye(groups, dtype=np.float32)
    pick = np.stack(
        [
            np.kron(eye, (z[None, :] == r[:, None]).astype(np.float32)),
            np.kron(eye, (z[None, :] == cells - 3 + r[:, None]).astype(np.float32)),
        ]
    )
    span = np.concatenate(
        [
            np.kron(eye, coef(z[None, :] - z[:, None])),
            np.kron(eye, coef(r[None, :] - 3 - z[:, None])),
            np.kron(eye, coef(cells + r[None, :] - z[:, None])),
        ],
        axis=1,
    )
    y = np.arange(lanes)
    diff = y[:, None] - y[None, :]
    wall = np.concatenate([coef(diff), coef(diff - lanes), coef(diff + lanes)], axis=0)
    owner = np.arange(snaps * cells) // cells
    one = (owner[:, None] == np.arange(snaps)[None, :]).astype(np.float32)
    fold = np.concatenate([one, one], axis=1)
    spread = np.concatenate([np.zeros_like(one.T), one.T], axis=0)
    return [jnp.asarray(a.astype(ml_dtypes.bfloat16)) for a in (pick, span, wall, fold, spread)]


def dot(a, b):
    return jnp.dot(a, b, preferred_element_type=F32)


def eliminate(rows):
    groups = list(rows)
    count = len(groups)
    sub = lax.broadcasted_iota(jnp.int32, (8, 128), 0)
    for j in range(8 * count):
        b, r = divmod(j, 8)
        pivot_row = jnp.broadcast_to(groups[b][r : r + 1, :], (8, 128))
        inv = 1.0 / jnp.broadcast_to(pivot_row[:, j : j + 1], (8, 128))
        scaled = pivot_row * inv
        for i in range(b, count):
            if i == b and r == 7:
                continue
            column = jnp.broadcast_to(groups[i][:, j : j + 1], (8, 128))
            if i == b:
                column = jnp.where(sub > r, column, 0.0)
            groups[i] = groups[i] - column * scaled
    return groups


def kernel(
    span_count, wall_count, total_rows,
    vel, metric_hbm, pick_hbm, span_hbm, wall_hbm, fold_hbm, spread_hbm,
    out_ref, r_ref,
    metric_ref, pick_ref, span_ref, wall_ref, fold_ref, spread_ref,
    u_buf, vw_buf, send_buf, lo_buf, hi_buf, ylo_buf, yhi_buf, acc, vort, prod,
    wall_sum, span_sum,
    local_sem, hs_sem, hr_sem, ys_sem, yr_sem, ws_sem, wr_sem, ss_sem, sr_sem,
):
    snaps = vel.shape[0]
    planes = u_buf.shape[1]
    cells, lanes = vel.shape[3], vel.shape[4]
    block = 16
    rows = block * planes * cells
    edge = block * planes * 3
    blocks = snaps // block
    me = lax.axis_index("span")
    mw = lax.axis_index("wall")

    load_u = pltpu.make_async_copy(vel.at[:, 0, pl.ds(3, planes)], u_buf, local_sem.at[0])
    load_v = pltpu.make_async_copy(vel.at[:, 1], vw_buf.at[0], local_sem.at[1])
    load_w = pltpu.make_async_copy(vel.at[:, 2], vw_buf.at[1], local_sem.at[2])
    load_pick = pltpu.make_async_copy(pick_hbm, pick_ref, local_sem.at[3])
    load_u.start()
    load_pick.start()
    load_v.start()
    load_w.start()
    loads = [
        pltpu.make_async_copy(src, dst, local_sem.at[4 + i])
        for i, (src, dst) in enumerate(
            (
                (wall_hbm, wall_ref),
                (metric_hbm, metric_ref),
                (span_hbm, span_ref),
                (fold_hbm, fold_ref),
                (spread_hbm, spread_ref),
            )
        )
    ]
    for load in loads:
        load.start()

    barrier = pltpu.get_barrier_semaphore()
    for d in range(1, span_count):
        pl.semaphore_signal(
            barrier, inc=1, device_id=(lax.rem(me + d, span_count), mw), device_id_type=MESH
        )
    for d in range(1, wall_count):
        pl.semaphore_signal(
            barrier, inc=1, device_id=(me, lax.rem(mw + d, wall_count)), device_id_type=MESH
        )

    def inner(c, k):
        at = pl.ds(k * block, block)
        if c == 0:
            value = u_buf[at]
        else:
            value = vw_buf[c - 1, at, pl.ds(3, planes)]
        return value.astype(F32).reshape(rows, lanes).astype(BF)

    load_pick.wait()
    load_u.wait()
    load_v.wait()
    for c in range(2):
        for k in range(blocks):
            f = inner(c, k)
            for side in range(2):
                send_buf[side, c, k * edge : (k + 1) * edge] = dot(pick_ref[side], f).astype(BF)
    load_w.wait()
    for load in loads:
        load.wait()
    pl.semaphore_wait(barrier, span_count + wall_count - 2)

    down = lax.rem(me + span_count - 1, span_count)
    up = lax.rem(me + 1, span_count)
    halo = []
    for c in range(2):
        to_down = pltpu.make_async_remote_copy(
            send_buf.at[0, c], hi_buf.at[c], hs_sem.at[0, c], hr_sem.at[0, c],
            device_id=(down, mw), device_id_type=MESH,
        )
        to_up = pltpu.make_async_remote_copy(
            send_buf.at[1, c], lo_buf.at[c], hs_sem.at[1, c], hr_sem.at[1, c],
            device_id=(up, mw), device_id_type=MESH,
        )
        to_down.start()
        to_up.start()
        halo.append((to_down, to_up))

    wall_src = (u_buf, vw_buf.at[1, :, pl.ds(3, planes)])
    y_up = [
        pltpu.make_async_remote_copy(
            wall_src[c], ylo_buf.at[c], ys_sem.at[0, c], yr_sem.at[0, c],
            device_id=(me, lax.rem(mw + 1, wall_count)), device_id_type=MESH,
        )
        for c in range(2)
    ]
    y_down = [
        pltpu.make_async_remote_copy(
            wall_src[c], yhi_buf.at[c], ys_sem.at[1, c], yr_sem.at[1, c],
            device_id=(me, lax.rem(mw + wall_count - 1, wall_count)), device_id_type=MESH,
        )
        for c in range(2)
    ]

    @pl.when(mw < wall_count - 1)
    def _():
        for c in range(2):
            y_up[c].start()

    @pl.when(mw > 0)
    def _():
        for c in range(2):
            y_down[c].start()

    @pl.when(mw == 0)
    def _():
        ylo_buf[...] = jnp.zeros_like(ylo_buf)

    @pl.when(mw == wall_count - 1)
    def _():
        yhi_buf[...] = jnp.zeros_like(yhi_buf)

    def along_x(k, carry):
        at = pl.ds(k * 4, 4)
        for c in range(2):
            f = [vw_buf[c, at, q].astype(F32) for q in range(6 + planes)]
            for p in range(planes):
                d = (
                    45.0 * (f[p + 4] - f[p + 2]) - 9.0 * (f[p + 5] - f[p + 1])
                    + (f[p + 6] - f[p])
                )
                if c == 0:
                    acc[2, p, at] = d
                else:
                    acc[1, p, at] = -d
        return carry

    lax.fori_loop(0, snaps // 4, along_x, 0)

    @pl.when(mw > 0)
    def _():
        for c in range(2):
            y_up[c].wait_recv()

    @pl.when(mw < wall_count - 1)
    def _():
        for c in range(2):
            y_down[c].wait_recv()

    metric = metric_ref[...].reshape(1, 1, 1, lanes)
    for c in range(2):
        for k in range(blocks):
            at = pl.ds(k * block, block)
            f = inner(2 * c, k)
            low = ylo_buf[c, at].astype(F32).reshape(rows, lanes).astype(BF)
            high = yhi_buf[c, at].astype(F32).reshape(rows, lanes).astype(BF)
            d = dot(jnp.concatenate([f, low, high], axis=1), wall_ref[...])
            d = d.reshape(block, planes, cells, lanes) * metric
            for p in range(planes):
                if c == 0:
                    acc[2, p, at] = acc[2, p, at] - d[:, p]
                else:
                    acc[0, p, at] = d[:, p]

    def finish(comp, p, k, value):
        slab = comp * planes + p
        vort[k * block * cells : (k + 1) * block * cells, slab * lanes : (slab + 1) * lanes] = (
            (value * (1.0 / 60.0)).reshape(block * cells, lanes).astype(BF)
        )

    for k in range(blocks):
        at = pl.ds(k * block, block)
        for p in range(planes):
            finish(2, p, k, acc[2, p, at])
    for c in range(2):
        halo[c][0].wait_recv()
        halo[c][1].wait_recv()
        for k in range(blocks):
            at = pl.ds(k * block, block)
            part = slice(k * edge, (k + 1) * edge)
            stack = jnp.concatenate([inner(c, k), lo_buf[c, part], hi_buf[c, part]], axis=0)
            d = dot(span_ref[...], stack).reshape(block, planes, cells, lanes)
            for p in range(planes):
                if c == 0:
                    finish(1, p, k, acc[1, p, at] + d[:, p])
                else:
                    finish(0, p, k, acc[0, p, at] - d[:, p])

    wide = snaps * cells
    tiles = wide // 128
    lane_z = lax.rem(lax.broadcasted_iota(jnp.int32, (snaps, 128), 1), cells)
    parts = []
    for t in range(tiles):
        prod[t] = lax.dot_general(
            vort[...], vort[t * 128 : (t + 1) * 128],
            (((1,), (1,)), ((), ())), preferred_element_type=F32,
        )
        q = jnp.zeros((snaps, 128), F32)
        for z in range(cells):
            q = jnp.where(lane_z == z, prod[t, pl.ds(z, snaps, stride=cells), :], q)
        parts.append(q)
    q = jnp.concatenate(parts, axis=1)
    q1 = q.astype(BF)
    rest = q - q1.astype(F32)
    q2 = rest.astype(BF)
    q3 = (rest - q2.astype(F32)).astype(BF)
    g3 = dot(jnp.concatenate([q1, q2, q3], axis=0), fold_ref[...])
    g = g3[:snaps] + g3[snaps : 2 * snaps] + g3[2 * snaps :]
    half = snaps // 2
    lane = lax.broadcasted_iota(jnp.int32, (half, 2 * snaps), 1)
    packed = jnp.where(lane < snaps, g[:half], g[half:])

    wall_sum[mw] = packed
    copies = []
    for d in range(1, wall_count):
        copy = pltpu.make_async_remote_copy(
            wall_sum.at[mw], wall_sum.at[mw], ws_sem.at[d], wr_sem.at[d],
            device_id=(me, lax.rem(mw + d, wall_count)), device_id_type=MESH,
        )
        copy.start()
        copies.append(copy)
    for copy in copies:
        copy.wait_recv()
    total = wall_sum[0]
    for i in range(1, wall_count):
        total = total + wall_sum[i]
    span_sum[me] = total
    for d in range(1, span_count):
        copy = pltpu.make_async_remote_copy(
            span_sum.at[me], span_sum.at[me], ss_sem.at[d], sr_sem.at[d],
            device_id=(lax.rem(me + d, span_count), mw), device_id_type=MESH,
        )
        copy.start()
        copies.append(copy)
    for copy in copies[wall_count - 1 :]:
        copy.wait_recv()
    total = span_sum[0]
    for i in range(1, span_count):
        total = total + span_sum[i]
    gram = total / total_rows

    sub = lax.broadcasted_iota(jnp.int32, (half, 2 * snaps), 0)
    top = jnp.where(lane < snaps, gram, (lane - snaps == sub).astype(F32))
    bottom = jnp.where(
        lane < snaps, pltpu.roll(gram, snaps, 1), (lane - snaps - half == sub).astype(F32)
    )
    groups = [top[8 * i : 8 * i + 8] for i in range(half // 8)]
    groups += [bottom[8 * i : 8 * i + 8] for i in range(half // 8)]
    done = jnp.concatenate(eliminate(groups), axis=0)
    lane = lax.broadcasted_iota(jnp.int32, (snaps, 2 * snaps), 1)
    sub = lax.broadcasted_iota(jnp.int32, (snaps, 2 * snaps), 0)
    diagonal = jnp.sum(jnp.where(lane == sub, done, 0.0), axis=1, keepdims=True)
    done = jnp.where(lane < sub, 0.0, done / jnp.sqrt(diagonal))
    r_ref[...] = done[:, :snaps]

    x = dot(done.astype(BF), spread_ref[...]).astype(BF)
    full = dot(fold_ref[:, :snaps], x)
    row_z = lax.rem(lax.broadcasted_iota(jnp.int32, (wide, wide), 0), cells)
    col_z = lax.rem(lax.broadcasted_iota(jnp.int32, (wide, wide), 1), cells)
    weights = jnp.where(row_z == col_z, full, 0.0).astype(BF)
    for comp in range(3):
        for p in range(planes):
            slab = comp * planes + p
            m = dot(weights, vort[:, slab * lanes : (slab + 1) * lanes])
            out_ref[:, comp, p] = m.reshape(snaps, cells, lanes).astype(BF)

    for copy in copies:
        copy.wait_send()
    for pair in halo:
        for copy in pair:
            copy.wait_send()

    @pl.when(mw < wall_count - 1)
    def _():
        for c in range(2):
            y_up[c].wait_send()

    @pl.when(mw > 0)
    def _():
        for c in range(2):
            y_down[c].wait_send()


def per_device(velocity, wall_metric):
    snaps, comps, depth, cells, lanes = velocity.shape
    planes = depth - 6
    spans, walls = lax.axis_size("span"), lax.axis_size("wall")
    total_rows = 3 * planes * cells * spans * lanes * walls
    consts = constants(snaps, cells, lanes, planes, 16)
    vmem = pl.BlockSpec(memory_space=pltpu.VMEM)
    dma = pltpu.SemaphoreType.DMA
    edge = snaps * planes * 3
    wide = snaps * cells
    return pl.pallas_call(
        functools.partial(kernel, spans, walls, total_rows),
        out_shape=(
            jax.ShapeDtypeStruct((snaps, 3, planes, cells, lanes), BF),
            jax.ShapeDtypeStruct((snaps, snaps), F32),
        ),
        in_specs=[pl.BlockSpec(memory_space=pl.ANY)] * 7,
        out_specs=(vmem, vmem),
        scratch_shapes=[
            pltpu.VMEM((1, lanes), F32),
            *[pltpu.VMEM(a.shape, a.dtype) for a in consts],
            pltpu.VMEM((snaps, planes, cells, lanes), BF),
            pltpu.VMEM((2, snaps, depth, cells, lanes), BF),
            pltpu.VMEM((2, 2, edge, lanes), BF),
            pltpu.VMEM((2, edge, lanes), BF),
            pltpu.VMEM((2, edge, lanes), BF),
            pltpu.VMEM((2, snaps, planes, cells, lanes), BF),
            pltpu.VMEM((2, snaps, planes, cells, lanes), BF),
            pltpu.VMEM((3, planes, snaps, cells, lanes), F32),
            pltpu.VMEM((wide, 3 * planes * lanes), BF),
            pltpu.VMEM((wide // 128, wide, 128), F32),
            pltpu.VMEM((walls, snaps // 2, 2 * snaps), F32),
            pltpu.VMEM((spans, snaps // 2, 2 * snaps), F32),
            dma((9,)),
            dma((2, 2)),
            dma((2, 2)),
            dma((2, 2)),
            dma((2, 2)),
            dma((walls,)),
            dma((walls,)),
            dma((spans,)),
            dma((spans,)),
        ],
        compiler_params=pltpu.CompilerParams(
            collective_id=0, has_side_effects=True, vmem_limit_bytes=60 << 20
        ),
        name="pod",
    )(velocity, wall_metric.reshape(1, lanes), *consts)


def solution(mesh):
    in_specs = (P(None, None, None, "span", "wall"), P("wall"))
    out_specs = (P(None, None, None, "span", "wall"), P())
    return jax.shard_map(
        per_device, mesh=mesh, in_specs=in_specs, out_specs=out_specs, check_vma=False
    )
```

```python
import functools

import jax
import jax.numpy as jnp
import ml_dtypes
import numpy as np
from jax import lax
from jax.experimental import pallas as pl
from jax.experimental.pallas import tpu as pltpu
from jax.sharding import PartitionSpec as P

MESH = pl.DeviceIdType.MESH
BF = jnp.bfloat16
F32 = jnp.float32


def coef(offset):
    table = {1: 45.0, 2: -9.0, 3: 1.0}
    size = np.abs(offset)
    out = np.zeros(offset.shape, np.float32)
    for step, value in table.items():
        out = np.where(size == step, value * np.sign(offset), out)
    return out


def constants(snaps, cells, lanes, planes, block):
    groups = block * planes
    z = np.arange(cells)
    r = np.arange(3)
    eye = np.eye(groups, dtype=np.float32)
    pick = np.stack(
        [
            np.kron(eye, (z[None, :] == r[:, None]).astype(np.float32)),
            np.kron(eye, (z[None, :] == cells - 3 + r[:, None]).astype(np.float32)),
        ]
    )
    span = np.concatenate(
        [
            np.kron(eye, coef(z[None, :] - z[:, None])),
            np.kron(eye, coef(r[None, :] - 3 - z[:, None])),
            np.kron(eye, coef(cells + r[None, :] - z[:, None])),
        ],
        axis=1,
    )
    y = np.arange(lanes)
    diff = y[:, None] - y[None, :]
    wall = coef(diff)
    packs = 2 * snaps // block
    step = lanes // packs
    gather = np.zeros((packs, lanes, lanes), np.float32)
    scatter = np.zeros((2, lanes, packs, lanes), np.float32)
    for g in range(packs):
        for t in range(3):
            gather[g, t, g * step + t] = 1.0
            gather[g, lanes - 3 + t, g * step + 3 + t] = 1.0
            scatter[0, g * step + 3 + t, g] = coef(t - 3 - y)
            scatter[1, g * step + t, g] = coef(lanes + t - y)
    gather = gather.reshape(packs * lanes, lanes)
    scatter = scatter.reshape(2 * lanes, packs * lanes)
    owner = np.arange(snaps * cells) // cells
    one = (owner[:, None] == np.arange(snaps)[None, :]).astype(np.float32)
    fold = np.concatenate([one, one], axis=1)
    spread = np.concatenate([np.zeros_like(one.T), one.T], axis=0)
    return [jnp.asarray(a.astype(ml_dtypes.bfloat16)) for a in (pick, gather, span, wall, scatter, fold, spread)]


def dot(a, b):
    return jnp.dot(a, b, preferred_element_type=F32)


def eliminate(rows):
    groups = list(rows)
    count = len(groups)
    sub = lax.broadcasted_iota(jnp.int32, (8, 128), 0)

    def wide(value):
        return jnp.broadcast_to(value, (8, 128))

    for b in range(count):
        at = 8 * b
        p = [wide(groups[b][k : k + 1, :]) for k in range(8)]
        s = {(k, l): wide(p[k][:, at + l : at + l + 1]) for k in range(8) for l in range(k, 8)}
        inv, f = [], {}
        for k in range(8):
            inv.append(1.0 / s[k, k])
            for l in range(k + 1, 8):
                f[k, l] = s[k, l] * inv[k]
                for m in range(l, 8):
                    s[l, m] = s[l, m] - f[k, l] * s[k, m]
        for k in range(8):
            for l in range(k + 1, 8):
                p[l] = p[l] - f[k, l] * p[k]
        scaled = [p[k] * inv[k] for k in range(8)]
        for i in range(b + 1, count):
            c = [wide(groups[i][:, at + k : at + k + 1]) for k in range(8)]
            value = groups[i]
            for k in range(8):
                for l in range(k + 1, 8):
                    c[l] = c[l] - c[k] * f[k, l]
                value = value - c[k] * scaled[k]
            groups[i] = value
        group = p[0]
        for k in range(1, 8):
            group = jnp.where(sub == k, p[k], group)
        groups[b] = group
    return groups


def kernel(
    span_count, near_count, wall_count, total_rows,
    vel, metric_hbm, pick_hbm, gather_hbm, span_hbm, wall_hbm, scatter_hbm, fold_hbm, spread_hbm,
    out_ref, r_ref,
    metric_ref, pick_ref, gather_ref, span_ref, wall_ref, scatter_ref, fold_ref, spread_ref,
    u_buf, vw_buf, send_buf, lo_buf, hi_buf, ysend_buf, ylo_buf, yhi_buf, acc, vort, prod,
    wall_sum, far_sum, near_sum,
    local_sem, hs_sem, hr_sem, ys_sem, yr_sem, ws_sem, wr_sem, fs_sem, fr_sem, ns_sem, nr_sem,
):
    snaps = vel.shape[0]
    planes = u_buf.shape[1]
    cells, lanes = vel.shape[3], vel.shape[4]
    block = 16
    rows = block * planes * cells
    edge = block * planes * 3
    blocks = snaps // block
    me = lax.axis_index("span")
    mw = lax.axis_index("wall")

    load_u = pltpu.make_async_copy(vel.at[:, 0, pl.ds(3, planes)], u_buf, local_sem.at[0])
    load_v = pltpu.make_async_copy(vel.at[:, 1], vw_buf.at[0], local_sem.at[1])
    load_w = pltpu.make_async_copy(vel.at[:, 2], vw_buf.at[1], local_sem.at[2])
    load_pick = pltpu.make_async_copy(pick_hbm, pick_ref, local_sem.at[3])
    load_u.start()
    load_pick.start()
    load_v.start()
    load_w.start()
    loads = [
        pltpu.make_async_copy(src, dst, local_sem.at[4 + i])
        for i, (src, dst) in enumerate(
            (
                (gather_hbm, gather_ref),
                (scatter_hbm, scatter_ref),
                (wall_hbm, wall_ref),
                (metric_hbm, metric_ref),
                (span_hbm, span_ref),
                (fold_hbm, fold_ref),
                (spread_hbm, spread_ref),
            )
        )
    ]
    for load in loads:
        load.start()

    barrier = pltpu.get_barrier_semaphore()
    far_count = span_count // near_count
    near, far = lax.rem(me, near_count), me // near_count

    def near_peer(d):
        return far * near_count + lax.rem(near + d, near_count)

    def far_peer(d):
        return lax.rem(far + d, far_count) * near_count + near

    down = lax.rem(me + span_count - 1, span_count)
    up = lax.rem(me + 1, span_count)
    peers = [down, up]
    peers += [near_peer(d) for d in range(1, near_count)]
    peers += [far_peer(d) for d in range(1, far_count)]
    for peer in peers:
        pl.semaphore_signal(barrier, inc=1, device_id=(peer, mw), device_id_type=MESH)
    for d in range(1, wall_count):
        pl.semaphore_signal(
            barrier, inc=1, device_id=(me, lax.rem(mw + d, wall_count)), device_id_type=MESH
        )

    def inner(c, k):
        at = pl.ds(k * block, block)
        if c == 0:
            value = u_buf[at]
        else:
            value = vw_buf[c - 1, at, pl.ds(3, planes)]
        return value.astype(F32).reshape(rows, lanes).astype(BF)

    load_pick.wait()
    load_u.wait()
    load_v.wait()
    for c in range(2):
        for k in range(blocks):
            f = inner(c, k)
            for side in range(2):
                send_buf[side, c, k * edge : (k + 1) * edge] = dot(pick_ref[side], f).astype(BF)
    load_w.wait()
    for load in loads:
        load.wait()
    ysend_buf[...] = dot(
        jnp.concatenate([inner(2 * c, k) for c in range(2) for k in range(blocks)], axis=1),
        gather_ref[...],
    ).astype(BF)
    pl.semaphore_wait(barrier, len(peers) + wall_count - 1)

    halo = []
    for c in range(2):
        to_down = pltpu.make_async_remote_copy(
            send_buf.at[0, c], hi_buf.at[c], hs_sem.at[0, c], hr_sem.at[0, c],
            device_id=(down, mw), device_id_type=MESH,
        )
        to_up = pltpu.make_async_remote_copy(
            send_buf.at[1, c], lo_buf.at[c], hs_sem.at[1, c], hr_sem.at[1, c],
            device_id=(up, mw), device_id_type=MESH,
        )
        to_down.start()
        to_up.start()
        halo.append((to_down, to_up))

    y_up = pltpu.make_async_remote_copy(
        ysend_buf, ylo_buf, ys_sem.at[0], yr_sem.at[0],
        device_id=(me, lax.rem(mw + 1, wall_count)), device_id_type=MESH,
    )
    y_down = pltpu.make_async_remote_copy(
        ysend_buf, yhi_buf, ys_sem.at[1], yr_sem.at[1],
        device_id=(me, lax.rem(mw + wall_count - 1, wall_count)), device_id_type=MESH,
    )

    @pl.when(mw < wall_count - 1)
    def _():
        y_up.start()

    @pl.when(mw > 0)
    def _():
        y_down.start()

    @pl.when(mw == 0)
    def _():
        ylo_buf[...] = jnp.zeros_like(ylo_buf)

    @pl.when(mw == wall_count - 1)
    def _():
        yhi_buf[...] = jnp.zeros_like(yhi_buf)

    def along_x(k, carry):
        at = pl.ds(k * 4, 4)
        for c in range(2):
            f = [vw_buf[c, at, q].astype(F32) for q in range(6 + planes)]
            for p in range(planes):
                d = (
                    45.0 * (f[p + 4] - f[p + 2]) - 9.0 * (f[p + 5] - f[p + 1])
                    + (f[p + 6] - f[p])
                )
                if c == 0:
                    acc[2, p, at] = d
                else:
                    acc[1, p, at] = -d
        return carry

    lax.fori_loop(0, snaps // 4, along_x, 0)

    @pl.when(mw > 0)
    def _():
        y_up.wait_recv()

    @pl.when(mw < wall_count - 1)
    def _():
        y_down.wait_recv()

    sides = jnp.concatenate([ylo_buf[...], yhi_buf[...]], axis=1)
    metric = metric_ref[...].reshape(1, 1, 1, lanes)
    for c in range(2):
        for k in range(blocks):
            at = pl.ds(k * block, block)
            f = inner(2 * c, k)
            g = c * blocks + k
            d = dot(f, wall_ref[...]) + dot(sides, scatter_ref[:, g * lanes : (g + 1) * lanes])
            d = d.reshape(block, planes, cells, lanes) * metric
            for p in range(planes):
                if c == 0:
                    acc[2, p, at] = acc[2, p, at] - d[:, p]
                else:
                    acc[0, p, at] = d[:, p]

    def finish(comp, p, k, value):
        slab = comp * planes + p
        vort[k * block * cells : (k + 1) * block * cells, slab * lanes : (slab + 1) * lanes] = (
            (value * (1.0 / 60.0)).reshape(block * cells, lanes).astype(BF)
        )

    for k in range(blocks):
        at = pl.ds(k * block, block)
        for p in range(planes):
            finish(2, p, k, acc[2, p, at])
    for c in range(2):
        halo[c][0].wait_recv()
        halo[c][1].wait_recv()
        for k in range(blocks):
            at = pl.ds(k * block, block)
            part = slice(k * edge, (k + 1) * edge)
            stack = jnp.concatenate([inner(c, k), lo_buf[c, part], hi_buf[c, part]], axis=0)
            d = dot(span_ref[...], stack).reshape(block, planes, cells, lanes)
            for p in range(planes):
                if c == 0:
                    finish(1, p, k, acc[1, p, at] + d[:, p])
                else:
                    finish(0, p, k, acc[0, p, at] - d[:, p])

    wide = snaps * cells
    tiles = wide // 128
    lane_z = lax.rem(lax.broadcasted_iota(jnp.int32, (snaps, 128), 1), cells)
    parts = []
    for t in range(tiles):
        prod[t] = lax.dot_general(
            vort[...], vort[t * 128 : (t + 1) * 128],
            (((1,), (1,)), ((), ())), preferred_element_type=F32,
        )
        q = jnp.zeros((snaps, 128), F32)
        for z in range(cells):
            q = jnp.where(lane_z == z, prod[t, pl.ds(z, snaps, stride=cells), :], q)
        parts.append(q)
    q = jnp.concatenate(parts, axis=1)
    q1 = q.astype(BF)
    rest = q - q1.astype(F32)
    q2 = rest.astype(BF)
    q3 = (rest - q2.astype(F32)).astype(BF)
    g3 = dot(jnp.concatenate([q1, q2, q3], axis=0), fold_ref[...])
    g = g3[:snaps] + g3[snaps : 2 * snaps] + g3[2 * snaps :]
    half = snaps // 2
    lane = lax.broadcasted_iota(jnp.int32, (half, 2 * snaps), 1)
    packed = jnp.where(lane < snaps, g[:half], g[half:])

    copies = []

    def gather_sum(value, buf, mine, count, send, recv, device):
        buf[mine] = value
        started = []
        for d in range(1, count):
            copy = pltpu.make_async_remote_copy(
                buf.at[mine], buf.at[mine], send.at[d], recv.at[d],
                device_id=device(d), device_id_type=MESH,
            )
            copy.start()
            started.append(copy)
        for copy in started:
            copy.wait_recv()
        copies.extend(started)
        total = buf[0]
        for i in range(1, count):
            total = total + buf[i]
        return total

    total = gather_sum(
        packed, wall_sum, mw, wall_count, ws_sem, wr_sem,
        lambda d: (me, lax.rem(mw + d, wall_count)),
    )
    total = gather_sum(
        total, far_sum, far, far_count, fs_sem, fr_sem, lambda d: (far_peer(d), mw)
    )
    total = gather_sum(
        total, near_sum, near, near_count, ns_sem, nr_sem, lambda d: (near_peer(d), mw)
    )
    gram = total / total_rows

    sub = lax.broadcasted_iota(jnp.int32, (half, 2 * snaps), 0)
    top = jnp.where(lane < snaps, gram, (lane - snaps == sub).astype(F32))
    bottom = jnp.where(
        lane < snaps, pltpu.roll(gram, snaps, 1), (lane - snaps - half == sub).astype(F32)
    )
    groups = [top[8 * i : 8 * i + 8] for i in range(half // 8)]
    groups += [bottom[8 * i : 8 * i + 8] for i in range(half // 8)]
    done = jnp.concatenate(eliminate(groups), axis=0)
    lane = lax.broadcasted_iota(jnp.int32, (snaps, 2 * snaps), 1)
    sub = lax.broadcasted_iota(jnp.int32, (snaps, 2 * snaps), 0)
    diagonal = jnp.sum(jnp.where(lane == sub, done, 0.0), axis=1, keepdims=True)
    done = jnp.where(lane < sub, 0.0, done / jnp.sqrt(diagonal))
    r_ref[...] = done[:, :snaps]

    x = dot(done.astype(BF), spread_ref[...]).astype(BF)
    full = dot(fold_ref[:, :snaps], x)
    row_z = lax.rem(lax.broadcasted_iota(jnp.int32, (wide, wide), 0), cells)
    col_z = lax.rem(lax.broadcasted_iota(jnp.int32, (wide, wide), 1), cells)
    weights = jnp.where(row_z == col_z, full, 0.0).astype(BF)
    for comp in range(3):
        for p in range(planes):
            slab = comp * planes + p
            m = dot(weights, vort[:, slab * lanes : (slab + 1) * lanes])
            out_ref[:, comp, p] = m.reshape(snaps, cells, lanes).astype(BF)

    for copy in copies:
        copy.wait_send()
    for pair in halo:
        for copy in pair:
            copy.wait_send()

    @pl.when(mw < wall_count - 1)
    def _():
        y_up.wait_send()

    @pl.when(mw > 0)
    def _():
        y_down.wait_send()


def per_device(velocity, wall_metric):
    snaps, comps, depth, cells, lanes = velocity.shape
    planes = depth - 6
    spans, walls = lax.axis_size("span"), lax.axis_size("wall")
    near = 1
    while spans % (2 * near) == 0 and 4 * near * near <= spans:
        near *= 2
    far = spans // near
    total_rows = 3 * planes * cells * spans * lanes * walls
    consts = constants(snaps, cells, lanes, planes, 16)
    vmem = pl.BlockSpec(memory_space=pltpu.VMEM)
    dma = pltpu.SemaphoreType.DMA
    edge = snaps * planes * 3
    wide = snaps * cells
    return pl.pallas_call(
        functools.partial(kernel, spans, near, walls, total_rows),
        out_shape=(
            jax.ShapeDtypeStruct((snaps, 3, planes, cells, lanes), BF),
            jax.ShapeDtypeStruct((snaps, snaps), F32),
        ),
        in_specs=[pl.BlockSpec(memory_space=pl.ANY)] * (2 + len(consts)),
        out_specs=(vmem, vmem),
        scratch_shapes=[
            pltpu.VMEM((1, lanes), F32),
            *[pltpu.VMEM(a.shape, a.dtype) for a in consts],
            pltpu.VMEM((snaps, planes, cells, lanes), BF),
            pltpu.VMEM((2, snaps, depth, cells, lanes), BF),
            pltpu.VMEM((2, 2, edge, lanes), BF),
            pltpu.VMEM((2, edge, lanes), BF),
            pltpu.VMEM((2, edge, lanes), BF),
            pltpu.VMEM((16 * planes * cells, lanes), BF),
            pltpu.VMEM((16 * planes * cells, lanes), BF),
            pltpu.VMEM((16 * planes * cells, lanes), BF),
            pltpu.VMEM((3, planes, snaps, cells, lanes), F32),
            pltpu.VMEM((wide, 3 * planes * lanes), BF),
            pltpu.VMEM((wide // 128, wide, 128), F32),
            pltpu.VMEM((walls, snaps // 2, 2 * snaps), F32),
            pltpu.VMEM((far, snaps // 2, 2 * snaps), F32),
            pltpu.VMEM((near, snaps // 2, 2 * snaps), F32),
            dma((11,)),
            dma((2, 2)),
            dma((2, 2)),
            dma((2,)),
            dma((2,)),
            dma((walls,)),
            dma((walls,)),
            dma((far,)),
            dma((far,)),
            dma((near,)),
            dma((near,)),
        ],
        compiler_params=pltpu.CompilerParams(
            collective_id=0, has_side_effects=True, vmem_limit_bytes=60 << 20
        ),
        name="pod",
    )(velocity, wall_metric.reshape(1, lanes), *consts)


def solution(mesh):
    in_specs = (P(None, None, None, "span", "wall"), P("wall"))
    out_specs = (P(None, None, None, "span", "wall"), P())
    return jax.shard_map(
        per_device, mesh=mesh, in_specs=in_specs, out_specs=out_specs, check_vma=False
    )
```

```python
import functools

import jax
import jax.numpy as jnp
import ml_dtypes
import numpy as np
from jax import lax
from jax.experimental import pallas as pl
from jax.experimental.pallas import tpu as pltpu
from jax.sharding import PartitionSpec as P

MESH = pl.DeviceIdType.MESH
BF = jnp.bfloat16
F32 = jnp.float32


def coef(offset):
    table = {1: 45.0, 2: -9.0, 3: 1.0}
    size = np.abs(offset)
    out = np.zeros(offset.shape, np.float32)
    for step, value in table.items():
        out = np.where(size == step, value * np.sign(offset), out)
    return out


def constants(snaps, cells, lanes, planes, block):
    groups = block * planes
    z = np.arange(cells)
    r = np.arange(3)
    eye = np.eye(groups, dtype=np.float32)
    pick = np.stack(
        [
            np.kron(eye, (z[None, :] == r[:, None]).astype(np.float32)),
            np.kron(eye, (z[None, :] == cells - 3 + r[:, None]).astype(np.float32)),
        ]
    )
    span = np.concatenate(
        [
            np.kron(eye, coef(z[None, :] - z[:, None])),
            np.kron(eye, coef(r[None, :] - 3 - z[:, None])),
            np.kron(eye, coef(cells + r[None, :] - z[:, None])),
        ],
        axis=1,
    )
    y = np.arange(lanes)
    diff = y[:, None] - y[None, :]
    wall = coef(diff)
    packs = 2 * snaps // block
    step = lanes // packs
    gather = np.zeros((packs, lanes, lanes), np.float32)
    scatter = np.zeros((2, lanes, packs, lanes), np.float32)
    for g in range(packs):
        for t in range(3):
            gather[g, t, g * step + t] = 1.0
            gather[g, lanes - 3 + t, g * step + 3 + t] = 1.0
            scatter[0, g * step + 3 + t, g] = coef(t - 3 - y)
            scatter[1, g * step + t, g] = coef(lanes + t - y)
    gather = gather.reshape(packs * lanes, lanes)
    scatter = scatter.reshape(2 * lanes, packs * lanes)
    owner = np.arange(snaps * cells) // cells
    one = (owner[:, None] == np.arange(snaps)[None, :]).astype(np.float32)
    fold = np.concatenate([one, one], axis=1)
    spread = np.concatenate([np.zeros_like(one.T), one.T], axis=0)
    return [jnp.asarray(a.astype(ml_dtypes.bfloat16)) for a in (pick, gather, span, wall, scatter, fold, spread)]


def dot(a, b):
    return jnp.dot(a, b, preferred_element_type=F32)


def eliminate(rows):
    groups = list(rows)
    count = len(groups)
    sub = lax.broadcasted_iota(jnp.int32, (8, 128), 0)

    def wide(value):
        return jnp.broadcast_to(value, (8, 128))

    for b in range(count):
        at = 8 * b
        p = [wide(groups[b][k : k + 1, :]) for k in range(8)]
        s = {(k, l): wide(p[k][:, at + l : at + l + 1]) for k in range(8) for l in range(k, 8)}
        inv, f = [], {}
        for k in range(8):
            inv.append(1.0 / s[k, k])
            for l in range(k + 1, 8):
                f[k, l] = s[k, l] * inv[k]
                for m in range(l, 8):
                    s[l, m] = s[l, m] - f[k, l] * s[k, m]
        for k in range(8):
            for l in range(k + 1, 8):
                p[l] = p[l] - f[k, l] * p[k]
        scaled = [p[k] * inv[k] for k in range(8)]
        for i in range(b + 1, count):
            c = [wide(groups[i][:, at + k : at + k + 1]) for k in range(8)]
            value = groups[i]
            for k in range(8):
                for l in range(k + 1, 8):
                    c[l] = c[l] - c[k] * f[k, l]
                value = value - c[k] * scaled[k]
            groups[i] = value
        group = p[0]
        for k in range(1, 8):
            group = jnp.where(sub == k, p[k], group)
        groups[b] = group
    return groups


def kernel(
    span_count, near_count, wall_count, total_rows,
    vel, metric_hbm, pick_hbm, gather_hbm, span_hbm, wall_hbm, scatter_hbm, fold_hbm, spread_hbm,
    vort, done_ref,
    metric_ref, pick_ref, gather_ref, span_ref, wall_ref, scatter_ref, fold_ref, spread_ref,
    u_buf, vw_buf, send_buf, lo_buf, hi_buf, ysend_buf, ylo_buf, yhi_buf, acc, prod,
    wall_sum, far_sum, near_sum,
    local_sem, hs_sem, hr_sem, ys_sem, yr_sem, ws_sem, wr_sem, fs_sem, fr_sem, ns_sem, nr_sem,
):
    snaps = vel.shape[0]
    planes = u_buf.shape[1]
    cells, lanes = vel.shape[3], vel.shape[4]
    block = 16
    rows = block * planes * cells
    edge = block * planes * 3
    blocks = snaps // block
    me = lax.axis_index("span")
    mw = lax.axis_index("wall")

    load_u = pltpu.make_async_copy(vel.at[:, 0, pl.ds(3, planes)], u_buf, local_sem.at[0])
    load_v = pltpu.make_async_copy(vel.at[:, 1], vw_buf.at[0], local_sem.at[1])
    load_w = pltpu.make_async_copy(vel.at[:, 2], vw_buf.at[1], local_sem.at[2])
    load_pick = pltpu.make_async_copy(pick_hbm, pick_ref, local_sem.at[3])
    load_u.start()
    load_pick.start()
    load_v.start()
    load_w.start()
    loads = [
        pltpu.make_async_copy(src, dst, local_sem.at[4 + i])
        for i, (src, dst) in enumerate(
            (
                (gather_hbm, gather_ref),
                (scatter_hbm, scatter_ref),
                (wall_hbm, wall_ref),
                (metric_hbm, metric_ref),
                (span_hbm, span_ref),
                (fold_hbm, fold_ref),
                (spread_hbm, spread_ref),
            )
        )
    ]
    for load in loads:
        load.start()

    barrier = pltpu.get_barrier_semaphore()
    far_count = span_count // near_count
    near, far = lax.rem(me, near_count), me // near_count

    def near_peer(d):
        return far * near_count + lax.rem(near + d, near_count)

    def far_peer(d):
        return lax.rem(far + d, far_count) * near_count + near

    down = lax.rem(me + span_count - 1, span_count)
    up = lax.rem(me + 1, span_count)
    peers = [down, up]
    peers += [near_peer(d) for d in range(1, near_count)]
    peers += [far_peer(d) for d in range(1, far_count)]
    for peer in peers:
        pl.semaphore_signal(barrier, inc=1, device_id=(peer, mw), device_id_type=MESH)
    for d in range(1, wall_count):
        pl.semaphore_signal(
            barrier, inc=1, device_id=(me, lax.rem(mw + d, wall_count)), device_id_type=MESH
        )

    def inner(c, k):
        at = pl.ds(k * block, block)
        if c == 0:
            value = u_buf[at]
        else:
            value = vw_buf[c - 1, at, pl.ds(3, planes)]
        return value.astype(F32).reshape(rows, lanes).astype(BF)

    load_pick.wait()
    load_u.wait()
    load_v.wait()
    for c in range(2):
        for k in range(blocks):
            f = inner(c, k)
            for side in range(2):
                send_buf[side, c, k * edge : (k + 1) * edge] = dot(pick_ref[side], f).astype(BF)
    load_w.wait()
    for load in loads:
        load.wait()
    ysend_buf[...] = dot(
        jnp.concatenate([inner(2 * c, k) for c in range(2) for k in range(blocks)], axis=1),
        gather_ref[...],
    ).astype(BF)
    pl.semaphore_wait(barrier, len(peers) + wall_count - 1)

    halo = []
    for c in range(2):
        to_down = pltpu.make_async_remote_copy(
            send_buf.at[0, c], hi_buf.at[c], hs_sem.at[0, c], hr_sem.at[0, c],
            device_id=(down, mw), device_id_type=MESH,
        )
        to_up = pltpu.make_async_remote_copy(
            send_buf.at[1, c], lo_buf.at[c], hs_sem.at[1, c], hr_sem.at[1, c],
            device_id=(up, mw), device_id_type=MESH,
        )
        to_down.start()
        to_up.start()
        halo.append((to_down, to_up))

    y_up = pltpu.make_async_remote_copy(
        ysend_buf, ylo_buf, ys_sem.at[0], yr_sem.at[0],
        device_id=(me, lax.rem(mw + 1, wall_count)), device_id_type=MESH,
    )
    y_down = pltpu.make_async_remote_copy(
        ysend_buf, yhi_buf, ys_sem.at[1], yr_sem.at[1],
        device_id=(me, lax.rem(mw + wall_count - 1, wall_count)), device_id_type=MESH,
    )

    @pl.when(mw < wall_count - 1)
    def _():
        y_up.start()

    @pl.when(mw > 0)
    def _():
        y_down.start()

    @pl.when(mw == 0)
    def _():
        ylo_buf[...] = jnp.zeros_like(ylo_buf)

    @pl.when(mw == wall_count - 1)
    def _():
        yhi_buf[...] = jnp.zeros_like(yhi_buf)

    def along_x(k, carry):
        at = pl.ds(k * 4, 4)
        for c in range(2):
            f = [vw_buf[c, at, q].astype(F32) for q in range(6 + planes)]
            for p in range(planes):
                d = (
                    45.0 * (f[p + 4] - f[p + 2]) - 9.0 * (f[p + 5] - f[p + 1])
                    + (f[p + 6] - f[p])
                )
                if c == 0:
                    acc[2, p, at] = d
                else:
                    acc[1, p, at] = -d
        return carry

    lax.fori_loop(0, snaps // 4, along_x, 0)

    @pl.when(mw > 0)
    def _():
        y_up.wait_recv()

    @pl.when(mw < wall_count - 1)
    def _():
        y_down.wait_recv()

    sides = jnp.concatenate([ylo_buf[...], yhi_buf[...]], axis=1)
    metric = metric_ref[...].reshape(1, 1, 1, lanes)
    for c in range(2):
        for k in range(blocks):
            at = pl.ds(k * block, block)
            f = inner(2 * c, k)
            g = c * blocks + k
            d = dot(f, wall_ref[...]) + dot(sides, scatter_ref[:, g * lanes : (g + 1) * lanes])
            d = d.reshape(block, planes, cells, lanes) * metric
            for p in range(planes):
                if c == 0:
                    acc[2, p, at] = acc[2, p, at] - d[:, p]
                else:
                    acc[0, p, at] = d[:, p]

    def finish(comp, p, k, value):
        slab = comp * planes + p
        vort[k * block * cells : (k + 1) * block * cells, slab * lanes : (slab + 1) * lanes] = (
            (value * (1.0 / 60.0)).reshape(block * cells, lanes).astype(BF)
        )

    for k in range(blocks):
        at = pl.ds(k * block, block)
        for p in range(planes):
            finish(2, p, k, acc[2, p, at])
    for c in range(2):
        halo[c][0].wait_recv()
        halo[c][1].wait_recv()
        for k in range(blocks):
            at = pl.ds(k * block, block)
            part = slice(k * edge, (k + 1) * edge)
            stack = jnp.concatenate([inner(c, k), lo_buf[c, part], hi_buf[c, part]], axis=0)
            d = dot(span_ref[...], stack).reshape(block, planes, cells, lanes)
            for p in range(planes):
                if c == 0:
                    finish(1, p, k, acc[1, p, at] + d[:, p])
                else:
                    finish(0, p, k, acc[0, p, at] - d[:, p])

    wide = snaps * cells
    tiles = wide // 128
    lane_z = lax.rem(lax.broadcasted_iota(jnp.int32, (snaps, 128), 1), cells)
    parts = []
    for t in range(tiles):
        prod[t] = lax.dot_general(
            vort[...], vort[t * 128 : (t + 1) * 128],
            (((1,), (1,)), ((), ())), preferred_element_type=F32,
        )
        q = jnp.zeros((snaps, 128), F32)
        for z in range(cells):
            q = jnp.where(lane_z == z, prod[t, pl.ds(z, snaps, stride=cells), :], q)
        parts.append(q)
    q = jnp.concatenate(parts, axis=1)
    q1 = q.astype(BF)
    rest = q - q1.astype(F32)
    q2 = rest.astype(BF)
    q3 = (rest - q2.astype(F32)).astype(BF)
    g3 = dot(jnp.concatenate([q1, q2, q3], axis=0), fold_ref[...])
    g = g3[:snaps] + g3[snaps : 2 * snaps] + g3[2 * snaps :]
    half = snaps // 2
    lane = lax.broadcasted_iota(jnp.int32, (half, 2 * snaps), 1)
    packed = jnp.where(lane < snaps, g[:half], g[half:])

    copies = []

    def gather_sum(value, buf, mine, count, send, recv, device):
        buf[mine] = value
        started = []
        for d in range(1, count):
            copy = pltpu.make_async_remote_copy(
                buf.at[mine], buf.at[mine], send.at[d], recv.at[d],
                device_id=device(d), device_id_type=MESH,
            )
            copy.start()
            started.append(copy)
        for copy in started:
            copy.wait_recv()
        copies.extend(started)
        total = buf[0]
        for i in range(1, count):
            total = total + buf[i]
        return total

    total = gather_sum(
        packed, wall_sum, mw, wall_count, ws_sem, wr_sem,
        lambda d: (me, lax.rem(mw + d, wall_count)),
    )
    total = gather_sum(
        total, far_sum, far, far_count, fs_sem, fr_sem, lambda d: (far_peer(d), mw)
    )
    total = gather_sum(
        total, near_sum, near, near_count, ns_sem, nr_sem, lambda d: (near_peer(d), mw)
    )
    gram = total / total_rows

    sub = lax.broadcasted_iota(jnp.int32, (half, 2 * snaps), 0)
    top = jnp.where(lane < snaps, gram, (lane - snaps == sub).astype(F32))
    bottom = jnp.where(
        lane < snaps, pltpu.roll(gram, snaps, 1), (lane - snaps - half == sub).astype(F32)
    )
    groups = [top[8 * i : 8 * i + 8] for i in range(half // 8)]
    groups += [bottom[8 * i : 8 * i + 8] for i in range(half // 8)]
    done = jnp.concatenate(eliminate(groups), axis=0)
    lane = lax.broadcasted_iota(jnp.int32, (snaps, 2 * snaps), 1)
    sub = lax.broadcasted_iota(jnp.int32, (snaps, 2 * snaps), 0)
    diagonal = jnp.sum(jnp.where(lane == sub, done, 0.0), axis=1, keepdims=True)
    done = jnp.where(lane < sub, 0.0, done / jnp.sqrt(diagonal))
    done_ref[...] = done

    for copy in copies:
        copy.wait_send()
    for pair in halo:
        for copy in pair:
            copy.wait_send()

    @pl.when(mw < wall_count - 1)
    def _():
        y_up.wait_send()

    @pl.when(mw > 0)
    def _():
        y_down.wait_send()


def modes_kernel(vort, done_ref, fold_ref, spread_ref, out_ref, r_ref):
    snaps, comps, planes, cells, lanes = out_ref.shape
    wide = snaps * cells
    done = done_ref[...]
    r_ref[...] = done[:, :snaps]
    x = dot(done.astype(BF), spread_ref[...]).astype(BF)
    full = dot(fold_ref[:, :snaps], x)
    row_z = lax.rem(lax.broadcasted_iota(jnp.int32, (wide, wide), 0), cells)
    col_z = lax.rem(lax.broadcasted_iota(jnp.int32, (wide, wide), 1), cells)
    weights = jnp.where(row_z == col_z, full, 0.0).astype(BF)
    for comp in range(comps):
        for p in range(planes):
            slab = comp * planes + p
            m = dot(weights, vort[:, slab * lanes : (slab + 1) * lanes])
            out_ref[:, comp, p] = m.reshape(snaps, cells, lanes).astype(BF)


def per_device(velocity, wall_metric):
    snaps, comps, depth, cells, lanes = velocity.shape
    planes = depth - 6
    spans, walls = lax.axis_size("span"), lax.axis_size("wall")
    near = 1
    while spans % (2 * near) == 0 and 4 * near * near <= spans:
        near *= 2
    far = spans // near
    total_rows = 3 * planes * cells * spans * lanes * walls
    consts = constants(snaps, cells, lanes, planes, 16)
    vmem = pl.BlockSpec(memory_space=pltpu.VMEM)
    dma = pltpu.SemaphoreType.DMA
    edge = snaps * planes * 3
    wide = snaps * cells
    vorticity, done = pl.pallas_call(
        functools.partial(kernel, spans, near, walls, total_rows),
        out_shape=(
            jax.ShapeDtypeStruct((wide, 3 * planes * lanes), BF),
            jax.ShapeDtypeStruct((snaps, 2 * snaps), F32),
        ),
        in_specs=[pl.BlockSpec(memory_space=pl.ANY)] * (2 + len(consts)),
        out_specs=(vmem, vmem),
        scratch_shapes=[
            pltpu.VMEM((1, lanes), F32),
            *[pltpu.VMEM(a.shape, a.dtype) for a in consts],
            pltpu.VMEM((snaps, planes, cells, lanes), BF),
            pltpu.VMEM((2, snaps, depth, cells, lanes), BF),
            pltpu.VMEM((2, 2, edge, lanes), BF),
            pltpu.VMEM((2, edge, lanes), BF),
            pltpu.VMEM((2, edge, lanes), BF),
            pltpu.VMEM((16 * planes * cells, lanes), BF),
            pltpu.VMEM((16 * planes * cells, lanes), BF),
            pltpu.VMEM((16 * planes * cells, lanes), BF),
            pltpu.VMEM((3, planes, snaps, cells, lanes), F32),
            pltpu.VMEM((wide // 128, wide, 128), F32),
            pltpu.VMEM((walls, snaps // 2, 2 * snaps), F32),
            pltpu.VMEM((far, snaps // 2, 2 * snaps), F32),
            pltpu.VMEM((near, snaps // 2, 2 * snaps), F32),
            dma((11,)),
            dma((2, 2)),
            dma((2, 2)),
            dma((2,)),
            dma((2,)),
            dma((walls,)),
            dma((walls,)),
            dma((far,)),
            dma((far,)),
            dma((near,)),
            dma((near,)),
        ],
        compiler_params=pltpu.CompilerParams(
            collective_id=0, has_side_effects=True, vmem_limit_bytes=60 << 20
        ),
        name="pod",
    )(velocity, wall_metric.reshape(1, lanes), *consts)
    return pl.pallas_call(
        modes_kernel,
        out_shape=(
            jax.ShapeDtypeStruct((snaps, 3, planes, cells, lanes), BF),
            jax.ShapeDtypeStruct((snaps, snaps), F32),
        ),
        in_specs=[vmem] * 4,
        out_specs=(vmem, vmem),
        name="modes",
    )(vorticity, done, *consts[-2:])


def solution(mesh):
    in_specs = (P(None, None, None, "span", "wall"), P("wall"))
    out_specs = (P(None, None, None, "span", "wall"), P())
    return jax.shard_map(
        per_device, mesh=mesh, in_specs=in_specs, out_specs=out_specs, check_vma=False
    )
```
